32 devices in a mesh: lat: 4 (over y, x), lon: 8 (over z, core).
Axes of the slice: x: 2, y: 2, z: 4, core: 2. Of those that a mesh axis runs over, the one named last changes fastest.
Arguments:
- field: float32 [80, 160, 384], P('lat', 'lon'), may hold values from -6 to 6
- lat_kernel: float32 [41], replicated, may hold values from 0.0121951215 to 0.036585364
- lon_kernel: float32 [41], replicated, may hold values from 0.0121951215 to 0.036585364
- time_taps: float32 [129], replicated, may hold values from -0.0058139535 to 0.0058139535
Outputs:
- basis: float32 [80, 160, 256], P('lat', 'lon')
- merged_factor: float32 [256, 256], replicated
The draws below stay inside these ranges and needn't reach their ends.
All inputs are finite; a program needn't handle non-finite values.
Results may differ from the reference program's by a relative error of at most 0.00016.
Values sent between devices are 32-bit elements; how exact they have to be, the bound alone decides.
A program may use at most 64 MiB of HBM per device.

```python
import jax
import jax.numpy as jnp
from jax import lax

TH = 64
SH = 20
TIN = 384
NLAT = 80
NLON = 160


def block_levels(rng, shape, pieces, smallest, top_value):
    level = 1.0
    for axis_at, shards_of in pieces:
        steps = jax.random.uniform(jax.random.fold_in(jax.random.fold_in(rng, 6), axis_at), (shards_of,), jnp.float32, smallest / len(pieces), top_value / len(pieces))
        level = level * jnp.repeat(jnp.exp(steps), shape[axis_at] // shards_of).reshape((-1,) + (1,) * (len(shape) - 1 - axis_at))
    return level


def normal_values(own_key, shape, spread, limit, cuts=(), kind=jnp.bfloat16):
    result = jax.random.normal(own_key, shape, jnp.float32) * spread
    if len(cuts) > 0:
        result = block_levels(own_key, shape, cuts, -0.22, 0.18) * result
    return jnp.clip(result, min=-limit, max=limit).astype(kind)


def setup_inputs(seed: int = 0) -> dict:
    arg_keys = jax.random.split(jax.random.key(seed), 5)
    return {
        "field": normal_values(arg_keys[0], (NLAT, NLON, TIN), 1.0, 6.0, ((0, 4), (1, 8)), jnp.float32),
        "lat_kernel": jnp.clip(jax.random.uniform(arg_keys[1], (2 * SH + 1,), jnp.float32, 0.0121951215, 0.036585364), 0.0121951215, 0.036585364),
        "lon_kernel": jnp.clip(jax.random.uniform(arg_keys[2], (2 * SH + 1,), jnp.float32, 0.0121951215, 0.036585364), 0.0121951215, 0.036585364),
        "time_taps": jnp.clip(jax.random.uniform(arg_keys[3], (2 * TH + 1,), jnp.float32, -0.0058139535, 0.0058139535), -0.0058139535, 0.0058139535),
    }


def reference(field, lat_kernel, lon_kernel, time_taps):
    nrows, ncols, length_in = field.shape
    steps_out = length_in - 2 * TH
    source = lax.broadcasted_iota(jnp.int32, (length_in, steps_out), 0)
    target = lax.broadcasted_iota(jnp.int32, (length_in, steps_out), 1)
    offset = source - target
    inside = (offset >= 0) & (offset <= 2 * TH)
    toeplitz = jnp.where(inside, time_taps[jnp.clip(offset, 0, 2 * TH)], jnp.float32(0.0))
    toeplitz = toeplitz + jnp.where(offset == TH, jnp.float32(1.0), jnp.float32(0.0))
    filtered = jnp.dot(field.reshape(-1, length_in).astype(jnp.float32), toeplitz.astype(jnp.float32), precision=lax.Precision.HIGHEST, preferred_element_type=jnp.float32).reshape(nrows, ncols, steps_out)
    padded = jnp.pad(filtered, ((SH, SH), (0, 0), (0, 0)))
    lat_done = jnp.zeros_like(filtered)
    for shift_k in range(2 * SH + 1):
        lat_done = lat_done + lat_kernel[shift_k] * padded[shift_k:shift_k + nrows]
    wrapped = jnp.concatenate([lat_done[:, ncols - SH:], lat_done, lat_done[:, :SH]], axis=1)
    smooth = jnp.zeros_like(filtered)
    for shift_k in range(2 * SH + 1):
        smooth = smooth + lon_kernel[shift_k] * wrapped[:, shift_k:shift_k + ncols]
    latitude = jnp.pi * (jnp.arange(nrows, dtype=jnp.float32) + 0.5) / nrows - jnp.pi / 2
    weights = jnp.sqrt(jnp.cos(latitude))
    matrix = (smooth * weights[:, None, None]).reshape(-1, steps_out)
    gram = lax.dot_general(matrix.astype(jnp.float32), matrix.astype(jnp.float32), (((0,), (0,)), ((), ())), precision=lax.Precision.HIGHEST, preferred_element_type=jnp.float32)
    lower = jnp.linalg.cholesky(gram)
    scale = jnp.sqrt(jnp.float32(nrows * ncols))
    solved = lax.linalg.triangular_solve(lower, matrix, left_side=False, lower=True, transpose_a=True)
    basis = (solved * scale).reshape(nrows, ncols, steps_out)
    return (basis, lower.T / scale)
```

```python
import functools

import jax
import jax.numpy as jnp
from jax import lax
from jax.experimental import pallas as pl
from jax.experimental.pallas import tpu as pltpu
from jax.sharding import PartitionSpec as P

TH = 64
SH = 20


def extended_2(value, sides, width, wrap):
    for axis, dim in sides:
        peers, length = (lax.axis_size(axis), value.shape[dim])
        up = [(i, (i + 1) % peers) for i in range(peers if wrap else peers - 1)]
        down = [(j, i) for i, j in up]
        last = lax.slice_in_dim(value, length - width, length, axis=dim)
        initial = lax.slice_in_dim(value, 0, width, axis=dim)
        before = lax.ppermute(last, axis, up)
        after = lax.ppermute(initial, axis, down)
        value = jnp.concatenate([before, value, after], axis=dim)
    return value


def skewed(coeffs, count, width):
    period = jnp.pad(coeffs, (0, count))
    flat = jnp.tile(period, count)[: count * width]
    return flat.reshape(count, width)


def banded(kernel, count):
    return skewed(kernel, count, count + 2 * SH)


def smooth_rows(band, extended):
    rows_in, cols_in, hours = extended.shape
    flat = extended.reshape(rows_in, cols_in * hours)
    result = jnp.dot(
        band, flat, precision=lax.Precision.HIGHEST, preferred_element_type=jnp.float32
    )
    return result.reshape(band.shape[0], cols_in, hours)


MESH = pl.DeviceIdType.MESH
NB = 32
LANES = 128


def sum_kernel(n_lat, n_lon, pair, g_ref, out_ref, rbuf, zbuf, ssem, rsem, zssem, zrsem, cssem, crsem):
    lat, lon = lax.axis_index("lat"), lax.axis_index("lon")
    n_p, n_z = n_lat * pair, n_lon // pair
    rows = g_ref.shape[0] // n_p
    core, z = lax.rem(lon, pair), lon // pair
    me = lat * pair + core

    def plane_peer(o):
        peer = lax.rem(me + o, n_p)
        return peer, (peer // pair, z * pair + lax.rem(peer, pair))

    def z_peer(o):
        return (lat, lax.rem(z + o, n_z) * pair + core)

    barrier = pltpu.get_barrier_semaphore()
    for o in range(1, n_p):
        pl.semaphore_signal(barrier, inc=1, device_id=plane_peer(o)[1], device_id_type=MESH)
    for o in range(1, n_z):
        pl.semaphore_signal(barrier, inc=1, device_id=z_peer(o), device_id_type=MESH)
    pl.semaphore_wait(barrier, n_p + n_z - 2)

    copies = []
    for o in range(1, n_p):
        peer, dev = plane_peer(o)
        c = pltpu.make_async_remote_copy(
            src_ref=g_ref.at[pl.ds(pl.multiple_of(peer * rows, 8), rows)], dst_ref=rbuf.at[o],
            send_sem=ssem.at[o], recv_sem=rsem.at[o], device_id=dev, device_id_type=MESH)
        c.start()
        copies.append(c)
    mine = pl.ds(pl.multiple_of(me * rows, 8), rows)
    acc = g_ref[mine, :]
    for o in range(1, n_p):
        copies[o - 1].wait_recv()
        acc = acc + rbuf[o]
    for c in copies:
        c.wait_send()
    zbuf[z] = acc

    copies = []
    for o in range(1, n_z):
        c = pltpu.make_async_remote_copy(
            src_ref=zbuf.at[z], dst_ref=zbuf.at[z],
            send_sem=zssem.at[o], recv_sem=zrsem.at[o], device_id=z_peer(o), device_id_type=MESH)
        c.start()
        copies.append(c)
    for c in copies:
        c.wait()
    total = zbuf[0]
    for k in range(1, n_z):
        total = total + zbuf[k]
    out_ref[mine, :] = total

    copies = []
    for o in range(1, n_p):
        c = pltpu.make_async_remote_copy(
            src_ref=out_ref.at[mine], dst_ref=out_ref.at[mine],
            send_sem=cssem.at[o], recv_sem=crsem.at[o], device_id=plane_peer(o)[1], device_id_type=MESH)
        c.start()
        copies.append(c)
    for c in copies:
        c.wait()


def sum_over_mesh(gram):
    n_lat, n_lon = lax.axis_size("lat"), lax.axis_size("lon")
    pair = 2 if n_lon % 2 == 0 else 1
    n_p, n_z = n_lat * pair, n_lon // pair
    if gram.shape[0] % (8 * n_p):
        return lax.psum(gram, ("lat", "lon"))
    rows, width = gram.shape[0] // n_p, gram.shape[1]
    dma = pltpu.SemaphoreType.DMA
    return pl.pallas_call(
        functools.partial(sum_kernel, n_lat, n_lon, pair),
        out_shape=jax.ShapeDtypeStruct(gram.shape, jnp.float32),
        in_specs=[pl.BlockSpec(memory_space=pltpu.VMEM)],
        out_specs=pl.BlockSpec(memory_space=pltpu.VMEM),
        scratch_shapes=[
            pltpu.VMEM((n_p, rows, width), jnp.float32),
            pltpu.VMEM((n_z, rows, width), jnp.float32),
            dma((n_p,)), dma((n_p,)), dma((n_z,)), dma((n_z,)), dma((n_p,)), dma((n_p,)),
        ],
        compiler_params=pltpu.CompilerParams(collective_id=0, has_side_effects=True),
        name="gram_sum",
    )(gram)


def factor_kernel(scale, g_ref, r_ref, y_ref, a, b):
    n = g_ref.shape[0]
    a[...] = g_ref[...]
    b[...] = (lax.broadcasted_iota(jnp.int32, (n, n), 0) == lax.broadcasted_iota(jnp.int32, (n, n), 1)).astype(jnp.float32)
    sub = lax.broadcasted_iota(jnp.int32, (8, LANES), 0)
    tiles = n // LANES
    for k in range(0, n, NB):
        kt = k // LANES
        live = [(a, t) for t in range(kt, tiles)] + [(b, t) for t in range(kt + 1)]
        grp = [[ref[k + 8 * h:k + 8 * h + 8, t * LANES:(t + 1) * LANES] for ref, t in live] for h in range(NB // 8)]
        for g in range(NB // 8):
            hs = range(g, NB // 8)
            lane = k + 8 * g - kt * LANES
            cols = [{h: jnp.broadcast_to(grp[h][0][:, lane + q:lane + q + 1], (8, LANES)) for h in hs} for q in range(8)]
            done = None
            for q in range(8):
                d = jnp.broadcast_to(cols[q][g][q:q + 1, :], (8, LANES))
                inv = 1.0 / d
                u = {h: cols[q][h] * inv for h in hs}
                u[g] = jnp.where(sub > q, u[g], 0.0)
                for p in range(q + 1, 8):
                    e = jnp.broadcast_to(cols[p][g][q:q + 1, :], (8, LANES))
                    for h in hs:
                        cols[p][h] = cols[p][h] - u[h] * e
                root = lax.sqrt(d)
                done = root if done is None else jnp.where(sub == q, root, done)
                for t in range(len(live)):
                    row = jnp.broadcast_to(grp[g][t][q:q + 1, :], (8, LANES))
                    for h in hs:
                        grp[h][t] = grp[h][t] - u[h] * row
            rinv = 1.0 / done
            for t in range(len(live)):
                grp[g][t] = grp[g][t] * rinv
        panel = jnp.concatenate([jnp.concatenate(x, axis=1) for x in grp], axis=0)
        n_a = tiles - kt
        row_id = lax.broadcasted_iota(jnp.int32, (NB, n_a * LANES), 0) + k
        lane_id = lax.broadcasted_iota(jnp.int32, (NB, n_a * LANES), 1) + kt * LANES
        pa = panel[:, :n_a * LANES]
        pb = panel[:, n_a * LANES:]
        if kt:
            r_ref[k:k + NB, :kt * LANES] = jnp.zeros((NB, kt * LANES), jnp.float32)
        r_ref[k:k + NB, kt * LANES:] = jnp.where(lane_id >= row_id, pa / scale, 0.0)
        y_ref[k:k + NB, :(kt + 1) * LANES] = pb * scale
        if kt + 1 < tiles:
            y_ref[k:k + NB, (kt + 1) * LANES:] = jnp.zeros((NB, n - (kt + 1) * LANES), jnp.float32)
        nxt = k + NB
        if nxt < n:
            nt = nxt // LANES
            left = panel[:, (nt - kt) * LANES:n_a * LANES]
            dims = (((0,), (0,)), ((), ()))
            right = panel[:, (nt - kt) * LANES:]
            upd = lax.dot_general(left, right, dims, precision=lax.Precision.HIGHEST, preferred_element_type=jnp.float32)
            upd = upd[nxt - nt * LANES:]
            w_a = n - nt * LANES
            a[nxt:, nt * LANES:] = a[nxt:, nt * LANES:] - upd[:, :w_a]
            b[nxt:, :(kt + 1) * LANES] = b[nxt:, :(kt + 1) * LANES] - upd[:, w_a:]


def factor(gram, scale):
    n = gram.shape[0]
    shape = jax.ShapeDtypeStruct((n, n), jnp.float32)
    vmem = pl.BlockSpec(memory_space=pltpu.VMEM)
    return pl.pallas_call(
        functools.partial(factor_kernel, scale),
        out_shape=(shape, shape),
        in_specs=[vmem],
        out_specs=(vmem, vmem),
        scratch_shapes=[pltpu.VMEM((n, n), jnp.float32)] * 2,
        name="factor",
    )(gram)


def body(field, lat_kernel, lon_kernel, time_taps):
    rows_lat, rows_lon, length_in = field.shape
    steps_out = length_in - 2 * TH
    lat_place = lax.axis_index("lat")
    total_lat = rows_lat * lax.axis_size("lat")
    cells = total_lat * rows_lon * lax.axis_size("lon")
    centre = (jnp.arange(2 * TH + 1, dtype=jnp.int32) == TH).astype(jnp.float32)
    taps_full = time_taps + centre
    skew_time = skewed(taps_full, steps_out, length_in)
    filtered = lax.dot_general(
        field.reshape(-1, length_in),
        skew_time,
        (((1,), (1,)), ((), ())),
        precision=lax.Precision.HIGHEST,
        preferred_element_type=jnp.float32,
    ).reshape(rows_lat, rows_lon, steps_out)
    lat_band = banded(lat_kernel, rows_lat)
    lon_band = banded(lon_kernel, rows_lon)
    extended = extended_2(filtered, (("lat", 0),), SH, False)
    narrow = smooth_rows(lat_band, extended)
    lat_done = extended_2(narrow, (("lon", 1),), SH, True)
    smooth = jnp.einsum(
        "jk,ikt->ijt",
        lon_band,
        lat_done,
        precision=lax.Precision.HIGHEST,
        preferred_element_type=jnp.float32,
    )
    globrow = (lat_place * rows_lat + jnp.arange(rows_lat, dtype=jnp.int32)).astype(jnp.float32)
    latitude = jnp.pi * (globrow + 0.5) / total_lat - jnp.pi / 2
    weights = jnp.sqrt(jnp.cos(latitude))
    matrix = (smooth * weights[:, None, None]).reshape(-1, steps_out)
    local_gram = lax.dot_general(
        matrix,
        matrix,
        (((0,), (0,)), ((), ())),
        precision=lax.Precision.HIGHEST,
        preferred_element_type=jnp.float32,
    )
    gram = sum_over_mesh(local_gram)
    upper, inverse = factor(gram, float(cells) ** 0.5)
    basis = lax.dot_general(
        matrix,
        inverse,
        (((1,), (1,)), ((), ())),
        precision=lax.Precision.HIGHEST,
        preferred_element_type=jnp.float32,
    ).reshape(rows_lat, rows_lon, steps_out)
    return (basis, upper)


def solution(mesh):
    placed = (P("lat", "lon", None), P(), P(), P())
    return jax.shard_map(
        body, mesh=mesh, in_specs=placed, out_specs=(P("lat", "lon", None), P()), check_vma=False
    )
```

```python
import functools

import jax
import jax.numpy as jnp
from jax import lax
from jax.experimental import pallas as pl
from jax.experimental.pallas import tpu as pltpu
from jax.sharding import PartitionSpec as P

TH = 64
SH = 20


def skewed(coeffs, count, width):
    period = jnp.pad(coeffs, (0, count))
    flat = jnp.tile(period, count)[: count * width]
    return flat.reshape(count, width)


MESH = pl.DeviceIdType.MESH
NB = 32
LANES = 128


def sum_kernel(n_lat, n_lon, pair, g_ref, out_ref, rbuf, zbuf, ssem, rsem, zssem, zrsem, cssem, crsem):
    lat, lon = lax.axis_index("lat"), lax.axis_index("lon")
    n_p, n_z = n_lat * pair, n_lon // pair
    rows = g_ref.shape[0] // n_p
    core, z = lax.rem(lon, pair), lon // pair
    me = lat * pair + core

    def plane_peer(o):
        peer = lax.rem(me + o, n_p)
        return peer, (peer // pair, z * pair + lax.rem(peer, pair))

    def z_peer(o):
        return (lat, lax.rem(z + o, n_z) * pair + core)

    barrier = pltpu.get_barrier_semaphore()
    for o in range(1, n_p):
        pl.semaphore_signal(barrier, inc=1, device_id=plane_peer(o)[1], device_id_type=MESH)
    for o in range(1, n_z):
        pl.semaphore_signal(barrier, inc=1, device_id=z_peer(o), device_id_type=MESH)
    pl.semaphore_wait(barrier, n_p + n_z - 2)

    copies = []
    for o in range(1, n_p):
        peer, dev = plane_peer(o)
        c = pltpu.make_async_remote_copy(
            src_ref=g_ref.at[pl.ds(pl.multiple_of(peer * rows, 8), rows)], dst_ref=rbuf.at[o],
            send_sem=ssem.at[o], recv_sem=rsem.at[o], device_id=dev, device_id_type=MESH)
        c.start()
        copies.append(c)
    mine = pl.ds(pl.multiple_of(me * rows, 8), rows)
    acc = g_ref[mine, :]
    for o in range(1, n_p):
        copies[o - 1].wait_recv()
        acc = acc + rbuf[o]
    for c in copies:
        c.wait_send()
    zbuf[z] = acc

    copies = []
    for o in range(1, n_z):
        c = pltpu.make_async_remote_copy(
            src_ref=zbuf.at[z], dst_ref=zbuf.at[z],
            send_sem=zssem.at[o], recv_sem=zrsem.at[o], device_id=z_peer(o), device_id_type=MESH)
        c.start()
        copies.append(c)
    for c in copies:
        c.wait()
    total = zbuf[0]
    for k in range(1, n_z):
        total = total + zbuf[k]
    out_ref[mine, :] = total

    copies = []
    for o in range(1, n_p):
        c = pltpu.make_async_remote_copy(
            src_ref=out_ref.at[mine], dst_ref=out_ref.at[mine],
            send_sem=cssem.at[o], recv_sem=crsem.at[o], device_id=plane_peer(o)[1], device_id_type=MESH)
        c.start()
        copies.append(c)
    for c in copies:
        c.wait()


def sum_over_mesh(gram):
    n_lat, n_lon = lax.axis_size("lat"), lax.axis_size("lon")
    pair = 2 if n_lon % 2 == 0 else 1
    n_p, n_z = n_lat * pair, n_lon // pair
    if gram.shape[0] % (8 * n_p):
        return lax.psum(gram, ("lat", "lon"))
    rows, width = gram.shape[0] // n_p, gram.shape[1]
    dma = pltpu.SemaphoreType.DMA
    return pl.pallas_call(
        functools.partial(sum_kernel, n_lat, n_lon, pair),
        out_shape=jax.ShapeDtypeStruct(gram.shape, jnp.float32),
        in_specs=[pl.BlockSpec(memory_space=pltpu.VMEM)],
        out_specs=pl.BlockSpec(memory_space=pltpu.VMEM),
        scratch_shapes=[
            pltpu.VMEM((n_p, rows, width), jnp.float32),
            pltpu.VMEM((n_z, rows, width), jnp.float32),
            dma((n_p,)), dma((n_p,)), dma((n_z,)), dma((n_z,)), dma((n_p,)), dma((n_p,)),
        ],
        compiler_params=pltpu.CompilerParams(collective_id=0, has_side_effects=True),
        name="gram_sum",
    )(gram)


def factor_kernel(scale, g_ref, r_ref, y_ref, a, b):
    n = g_ref.shape[0]
    a[...] = g_ref[...]
    b[...] = (lax.broadcasted_iota(jnp.int32, (n, n), 0) == lax.broadcasted_iota(jnp.int32, (n, n), 1)).astype(jnp.float32)
    sub = lax.broadcasted_iota(jnp.int32, (8, LANES), 0)
    tiles = n // LANES
    for k in range(0, n, NB):
        kt = k // LANES
        live = [(a, t) for t in range(kt, tiles)] + [(b, t) for t in range(kt + 1)]
        grp = [[ref[k + 8 * h:k + 8 * h + 8, t * LANES:(t + 1) * LANES] for ref, t in live] for h in range(NB // 8)]
        for g in range(NB // 8):
            hs = range(g, NB // 8)
            lane = k + 8 * g - kt * LANES
            cols = [{h: jnp.broadcast_to(grp[h][0][:, lane + q:lane + q + 1], (8, LANES)) for h in hs} for q in range(8)]
            done = None
            for q in range(8):
                d = jnp.broadcast_to(cols[q][g][q:q + 1, :], (8, LANES))
                inv = 1.0 / d
                u = {h: cols[q][h] * inv for h in hs}
                u[g] = jnp.where(sub > q, u[g], 0.0)
                for p in range(q + 1, 8):
                    e = jnp.broadcast_to(cols[p][g][q:q + 1, :], (8, LANES))
                    for h in hs:
                        cols[p][h] = cols[p][h] - u[h] * e
                root = lax.sqrt(d)
                done = root if done is None else jnp.where(sub == q, root, done)
                for t in range(len(live)):
                    row = jnp.broadcast_to(grp[g][t][q:q + 1, :], (8, LANES))
                    for h in hs:
                        grp[h][t] = grp[h][t] - u[h] * row
            rinv = 1.0 / done
            for t in range(len(live)):
                grp[g][t] = grp[g][t] * rinv
        panel = jnp.concatenate([jnp.concatenate(x, axis=1) for x in grp], axis=0)
        n_a = tiles - kt
        row_id = lax.broadcasted_iota(jnp.int32, (NB, n_a * LANES), 0) + k
        lane_id = lax.broadcasted_iota(jnp.int32, (NB, n_a * LANES), 1) + kt * LANES
        pa = panel[:, :n_a * LANES]
        pb = panel[:, n_a * LANES:]
        if kt:
            r_ref[k:k + NB, :kt * LANES] = jnp.zeros((NB, kt * LANES), jnp.float32)
        r_ref[k:k + NB, kt * LANES:] = jnp.where(lane_id >= row_id, pa / scale, 0.0)
        y_ref[k:k + NB, :(kt + 1) * LANES] = pb * scale
        if kt + 1 < tiles:
            y_ref[k:k + NB, (kt + 1) * LANES:] = jnp.zeros((NB, n - (kt + 1) * LANES), jnp.float32)
        nxt = k + NB
        if nxt < n:
            nt = nxt // LANES
            left = panel[:, (nt - kt) * LANES:n_a * LANES]
            dims = (((0,), (0,)), ((), ()))
            right = panel[:, (nt - kt) * LANES:]
            upd = lax.dot_general(left, right, dims, precision=lax.Precision.HIGHEST, preferred_element_type=jnp.float32)
            upd = upd[nxt - nt * LANES:]
            w_a = n - nt * LANES
            a[nxt:, nt * LANES:] = a[nxt:, nt * LANES:] - upd[:, :w_a]
            b[nxt:, :(kt + 1) * LANES] = b[nxt:, :(kt + 1) * LANES] - upd[:, w_a:]


def factor(gram, scale):
    n = gram.shape[0]
    shape = jax.ShapeDtypeStruct((n, n), jnp.float32)
    vmem = pl.BlockSpec(memory_space=pltpu.VMEM)
    return pl.pallas_call(
        functools.partial(factor_kernel, scale),
        out_shape=(shape, shape),
        in_specs=[vmem],
        out_specs=(vmem, vmem),
        scratch_shapes=[pltpu.VMEM((n, n), jnp.float32)] * 2,
        name="factor",
    )(gram)


def halo_kernel(n_lat, n_lon, cols, taps, pieces, x_ref, w_ref, out_ref, ext, shifted, psend, precv, fsend, frecv, lsend, lrecv):
    lat, lon = lax.axis_index("lat"), lax.axis_index("lon")
    chunks, size = x_ref.shape[0], x_ref.shape[1]
    odd = lax.rem(lat, 2)
    partner = lat + 1 - 2 * odd
    target = lat + 2 - 4 * odd
    source = lat - 2 + 4 * odd
    hands_on = jnp.logical_and(target >= 0, target < n_lat)
    gets = jnp.logical_and(source >= 0, source < n_lat)
    right, left = lax.rem(lon + 1, n_lon), lax.rem(lon + n_lon - 1, n_lon)
    step = size // pieces

    barrier = pltpu.get_barrier_semaphore()
    for dev in ((partner, lon), (lat, left), (lat, right)):
        pl.semaphore_signal(barrier, inc=1, device_id=dev, device_id_type=MESH)

    @pl.when(gets)
    def _():
        pl.semaphore_signal(barrier, inc=1, device_id=(source, lon), device_id_type=MESH)

    @pl.when(hands_on)
    def _():
        pl.semaphore_signal(barrier, inc=1, device_id=(target, lon), device_id_type=MESH)

    pl.semaphore_wait(barrier, 3 + gets.astype(jnp.int32) + hands_on.astype(jnp.int32))

    far = 2 * size * odd
    near = 2 * size * (1 - odd)

    def swap(c, s):
        return pltpu.make_async_remote_copy(
            src_ref=x_ref.at[c, pl.ds(s * step, step)],
            dst_ref=ext.at[c, pl.ds(pl.multiple_of(far + s * step, 8), step)],
            send_sem=psend.at[c, s], recv_sem=precv.at[c, s], device_id=(partner, lon), device_id_type=MESH)

    def hand(c, s):
        return pltpu.make_async_remote_copy(
            src_ref=ext.at[c, pl.ds(pl.multiple_of(near + s * step, 8), step)],
            dst_ref=ext.at[c, pl.ds(pl.multiple_of(far + s * step, 8), step)],
            send_sem=fsend.at[c, s], recv_sem=frecv.at[c, s], device_id=(target, lon), device_id_type=MESH)

    def side(c, way):
        return pltpu.make_async_remote_copy(
            src_ref=out_ref.at[c, 1], dst_ref=out_ref.at[c, 2 * way],
            send_sem=lsend.at[c, way], recv_sem=lrecv.at[c, way],
            device_id=(lat, left if way else right), device_id_type=MESH)

    def relay(c, s):
        swap(c, s).wait_recv()

        @pl.when(hands_on)
        def _():
            hand(c, s).start()

    for c in range(chunks):
        for s in range(pieces):
            swap(c, s).start()
    for c in range(chunks):
        ext[c, size:2 * size] = x_ref[c]

    @pl.when(jnp.logical_not(gets))
    def _():
        for c in range(chunks):
            ext[c, pl.ds(pl.multiple_of(far, 8), size)] = jnp.zeros((size, LANES), jnp.float32)

    rows_lat = size // cols
    classes = 1
    while classes * cols % 8:
        classes *= 2
    block = classes * cols
    order = [(c, s) for c in range(chunks) for s in range(pieces)]
    at = 0
    for c in range(chunks):
        ahead = min(len(order), (c + 1) * pieces + pieces // 2)
        for p in order[at:ahead]:
            relay(*p)
        at = ahead

        @pl.when(gets)
        def _():
            for s in range(pieces):
                hand(c, s).wait_recv()

        for q in range(1, classes):
            shifted[q - 1, :3 * size - q * cols] = ext[c, q * cols:]

        def smooth(b, carry):
            acc = None
            for k in range(taps):
                place = k + rows_lat - taps // 2
                q = place % classes
                rows = pl.ds(pl.multiple_of(b * block + (place - q) * cols, 8), block)
                value = ext[c, rows] if q == 0 else shifted[q - 1, rows]
                acc = w_ref[k] * value if acc is None else acc + w_ref[k] * value
            out_ref[c, 1, pl.ds(pl.multiple_of(b * block, 8), block)] = acc
            return carry

        lax.fori_loop(0, size // block, smooth, 0)
        side(c, 0).start()
        side(c, 1).start()
    for c in range(chunks):
        for s in range(pieces):
            swap(c, s).wait_send()

    @pl.when(hands_on)
    def _():
        for c in range(chunks):
            for s in range(pieces):
                hand(c, s).wait_send()

    for c in range(chunks):
        side(c, 0).wait()
        side(c, 1).wait()


def halo(tiles, lat_kernel, cols):
    n_lat, n_lon = lax.axis_size("lat"), lax.axis_size("lon")
    chunks, size, width = tiles.shape
    classes = 1
    while classes * cols % 8:
        classes *= 2
    pieces = next(p for p in (5, 4, 2, 1) if size % (8 * p) == 0)
    dma = pltpu.SemaphoreType.DMA
    vmem = pl.BlockSpec(memory_space=pltpu.VMEM)
    return pl.pallas_call(
        functools.partial(halo_kernel, n_lat, n_lon, cols, lat_kernel.shape[0], pieces),
        out_shape=jax.ShapeDtypeStruct((chunks, 3, size, width), jnp.float32),
        in_specs=[vmem, pl.BlockSpec(memory_space=pltpu.SMEM)],
        out_specs=vmem,
        scratch_shapes=[
            pltpu.VMEM((chunks, 3 * size, width), jnp.float32),
            pltpu.VMEM((max(1, classes - 1), 3 * size, width), jnp.float32),
        ] + [dma((chunks, pieces))] * 4 + [dma((chunks, 2))] * 2,
        compiler_params=pltpu.CompilerParams(collective_id=1, has_side_effects=True),
        name="halo",
    )(tiles, lat_kernel)


def gram_kernel(cols, group, x_ref, lon_ref, w_ref, m_ref, g_ref):
    chunks, parts, size, width = x_ref.shape
    taps = lon_ref.shape[0]
    rows = group * cols
    shape = (rows, parts * rows)
    r, e = lax.broadcasted_iota(jnp.int32, shape, 0), lax.broadcasted_iota(jnp.int32, shape, 1)
    part = sum((e >= p * rows).astype(jnp.int32) for p in range(1, parts)) + jnp.zeros(shape, jnp.int32)
    e = e - part * rows
    er = sum((e >= q * cols).astype(jnp.int32) for q in range(1, group)) + jnp.zeros(shape, jnp.int32)
    rr = sum((r >= q * cols).astype(jnp.int32) for q in range(1, group)) + jnp.zeros(shape, jnp.int32)
    offset = part * cols + (e - er * cols) - (r - rr * cols) - (cols - taps // 2)
    offset = jnp.where(er == rr, offset, -1)
    band = jnp.zeros(shape, jnp.float32)
    for k in range(taps):
        band = jnp.where(offset == k, lon_ref[k], band)
    which = rr[:, :1] + jnp.zeros((rows, chunks * width), jnp.int32)
    for g in range(size // rows):
        at = slice(g * rows, (g + 1) * rows)
        value = jnp.concatenate(
            [jnp.concatenate([x_ref[c, p, at] for c in range(chunks)], axis=1) for p in range(parts)], axis=0)
        value = jnp.dot(band, value, precision=lax.Precision.HIGHEST, preferred_element_type=jnp.float32)
        weight = jnp.zeros(value.shape, jnp.float32)
        for q in range(group):
            weight = jnp.where(which == q, w_ref[g * group + q], weight)
        m_ref[at] = value * weight
    g_ref[...] = lax.dot_general(
        m_ref[...], m_ref[...], (((0,), (0,)), ((), ())),
        precision=lax.Precision.HIGHEST, preferred_element_type=jnp.float32)


def matrix_and_gram(ext, lon_kernel, weights, cols):
    chunks, parts, size, width = ext.shape
    rows_lat = size // cols
    group = max(q for q in range(1, rows_lat + 1) if rows_lat % q == 0 and q * cols % 8 == 0 and (q * cols <= 96 or q == rows_lat))
    group = min([q for q in range(1, rows_lat + 1) if rows_lat % q == 0 and q * cols % 8 == 0 and 64 <= q * cols] or [group])
    vmem, smem = pl.BlockSpec(memory_space=pltpu.VMEM), pl.BlockSpec(memory_space=pltpu.SMEM)
    steps = chunks * width
    return pl.pallas_call(
        functools.partial(gram_kernel, cols, group),
        out_shape=(jax.ShapeDtypeStruct((size, steps), jnp.float32), jax.ShapeDtypeStruct((steps, steps), jnp.float32)),
        in_specs=[vmem, smem, smem],
        out_specs=(vmem, vmem),
        name="matrix_gram",
    )(ext, lon_kernel, weights)


def body(field, lat_kernel, lon_kernel, time_taps):
    rows_lat, rows_lon, length_in = field.shape
    steps_out = length_in - 2 * TH
    lat_place = lax.axis_index("lat")
    total_lat = rows_lat * lax.axis_size("lat")
    cells = total_lat * rows_lon * lax.axis_size("lon")
    centre = (jnp.arange(2 * TH + 1, dtype=jnp.int32) == TH).astype(jnp.float32)
    taps_full = time_taps + centre
    skew_time = skewed(taps_full, steps_out, length_in)
    flat = field.reshape(-1, length_in)
    tiles = jnp.stack([
        lax.dot_general(
            flat,
            skew_time[at:at + LANES],
            (((1,), (1,)), ((), ())),
            precision=lax.Precision.HIGHEST,
            preferred_element_type=jnp.float32,
        )
        for at in range(0, steps_out, LANES)
    ])
    ext = halo(tiles, lat_kernel, rows_lon)
    globrow = (lat_place * rows_lat + jnp.arange(rows_lat, dtype=jnp.int32)).astype(jnp.float32)
    latitude = jnp.pi * (globrow + 0.5) / total_lat - jnp.pi / 2
    weights = jnp.sqrt(jnp.cos(latitude))
    matrix, local_gram = matrix_and_gram(ext, lon_kernel, weights, rows_lon)
    gram = sum_over_mesh(local_gram)
    upper, inverse = factor(gram, float(cells) ** 0.5)
    basis = lax.dot_general(
        matrix,
        inverse,
        (((1,), (1,)), ((), ())),
        precision=lax.Precision.HIGHEST,
        preferred_element_type=jnp.float32,
    ).reshape(rows_lat, rows_lon, steps_out)
    return (basis, upper)


def solution(mesh):
    placed = (P("lat", "lon", None), P(), P(), P())
    return jax.shard_map(
        body, mesh=mesh, in_specs=placed, out_specs=(P("lat", "lon", None), P()), check_vma=False
    )
```

```python
import functools

import jax
import jax.numpy as jnp
import numpy as np
from jax import lax
from jax.experimental import pallas as pl
from jax.experimental.pallas import tpu as pltpu
from jax.sharding import PartitionSpec as P


MESH = pl.DeviceIdType.MESH
NB = 32
LANES = 128


def sum_kernel(n_lat, n_lon, pair, g_ref, out_ref, rbuf, zbuf, ssem, rsem, zssem, zrsem, cssem, crsem):
    lat, lon = lax.axis_index("lat"), lax.axis_index("lon")
    n_p, n_z = n_lat * pair, n_lon // pair
    rows = g_ref.shape[0] // n_p
    core, z = lax.rem(lon, pair), lon // pair
    me = lat * pair + core

    def plane_peer(o):
        peer = lax.rem(me + o, n_p)
        return peer, (peer // pair, z * pair + lax.rem(peer, pair))

    def z_peer(o):
        return (lat, lax.rem(z + o, n_z) * pair + core)

    barrier = pltpu.get_barrier_semaphore()
    for o in range(1, n_p):
        pl.semaphore_signal(barrier, inc=1, device_id=plane_peer(o)[1], device_id_type=MESH)
    for o in range(1, n_z):
        pl.semaphore_signal(barrier, inc=1, device_id=z_peer(o), device_id_type=MESH)
    pl.semaphore_wait(barrier, n_p + n_z - 2)

    copies = []
    for o in range(1, n_p):
        peer, dev = plane_peer(o)
        c = pltpu.make_async_remote_copy(
            src_ref=g_ref.at[pl.ds(pl.multiple_of(peer * rows, 8), rows)], dst_ref=rbuf.at[o],
            send_sem=ssem.at[o], recv_sem=rsem.at[o], device_id=dev, device_id_type=MESH)
        c.start()
        copies.append(c)
    mine = pl.ds(pl.multiple_of(me * rows, 8), rows)
    acc = g_ref[mine, :]
    for o in range(1, n_p):
        copies[o - 1].wait_recv()
        acc = acc + rbuf[o]
    for c in copies:
        c.wait_send()
    zbuf[z] = acc

    copies = []
    for o in range(1, n_z):
        c = pltpu.make_async_remote_copy(
            src_ref=zbuf.at[z], dst_ref=zbuf.at[z],
            send_sem=zssem.at[o], recv_sem=zrsem.at[o], device_id=z_peer(o), device_id_type=MESH)
        c.start()
        copies.append(c)
    for c in copies:
        c.wait()
    total = zbuf[0]
    for k in range(1, n_z):
        total = total + zbuf[k]
    out_ref[mine, :] = total

    copies = []
    for o in range(1, n_p):
        c = pltpu.make_async_remote_copy(
            src_ref=out_ref.at[mine], dst_ref=out_ref.at[mine],
            send_sem=cssem.at[o], recv_sem=crsem.at[o], device_id=plane_peer(o)[1], device_id_type=MESH)
        c.start()
        copies.append(c)
    for c in copies:
        c.wait()


def sum_over_mesh(gram):
    n_lat, n_lon = lax.axis_size("lat"), lax.axis_size("lon")
    pair = 2 if n_lon % 2 == 0 else 1
    n_p, n_z = n_lat * pair, n_lon // pair
    if gram.shape[0] % (8 * n_p):
        return lax.psum(gram, ("lat", "lon"))
    rows, width = gram.shape[0] // n_p, gram.shape[1]
    dma = pltpu.SemaphoreType.DMA
    return pl.pallas_call(
        functools.partial(sum_kernel, n_lat, n_lon, pair),
        out_shape=jax.ShapeDtypeStruct(gram.shape, jnp.float32),
        in_specs=[pl.BlockSpec(memory_space=pltpu.VMEM)],
        out_specs=pl.BlockSpec(memory_space=pltpu.VMEM),
        scratch_shapes=[
            pltpu.VMEM((n_p, rows, width), jnp.float32),
            pltpu.VMEM((n_z, rows, width), jnp.float32),
            dma((n_p,)), dma((n_p,)), dma((n_z,)), dma((n_z,)), dma((n_p,)), dma((n_p,)),
        ],
        compiler_params=pltpu.CompilerParams(collective_id=0, has_side_effects=True),
        name="gram_sum",
    )(gram)


def factor_kernel(scale, n, g_ref, m_ref, r_ref, basis_ref, a, b, y_ref):
    at = 0
    for t in range(0, n, LANES):
        if t:
            a[t:t + LANES, :t] = jnp.zeros((LANES, t), jnp.float32)
        for q in range(t, n, LANES):
            a[t:t + LANES, q:q + LANES] = g_ref[at:at + LANES]
            at += LANES
    b[...] = (lax.broadcasted_iota(jnp.int32, (n, n), 0) == lax.broadcasted_iota(jnp.int32, (n, n), 1)).astype(jnp.float32)
    sub = lax.broadcasted_iota(jnp.int32, (8, LANES), 0)
    tiles = n // LANES
    for k in range(0, n, NB):
        kt = k // LANES
        live = [(a, t) for t in range(kt, tiles)] + [(b, t) for t in range(kt + 1)]
        grp = [[ref[k + 8 * h:k + 8 * h + 8, t * LANES:(t + 1) * LANES] for ref, t in live] for h in range(NB // 8)]
        for g in range(NB // 8):
            hs = range(g, NB // 8)
            lane = k + 8 * g - kt * LANES
            cols = [{h: jnp.broadcast_to(grp[h][0][:, lane + q:lane + q + 1], (8, LANES)) for h in hs} for q in range(8)]
            done = None
            for q in range(8):
                d = jnp.broadcast_to(cols[q][g][q:q + 1, :], (8, LANES))
                inv = 1.0 / d
                u = {h: cols[q][h] * inv for h in hs}
                u[g] = jnp.where(sub > q, u[g], 0.0)
                for p in range(q + 1, 8):
                    e = jnp.broadcast_to(cols[p][g][q:q + 1, :], (8, LANES))
                    for h in hs:
                        cols[p][h] = cols[p][h] - u[h] * e
                root = lax.sqrt(d)
                done = root if done is None else jnp.where(sub == q, root, done)
                for t in range(len(live)):
                    row = jnp.broadcast_to(grp[g][t][q:q + 1, :], (8, LANES))
                    for h in hs:
                        grp[h][t] = grp[h][t] - u[h] * row
            rinv = 1.0 / done
            for t in range(len(live)):
                grp[g][t] = grp[g][t] * rinv
        panel = jnp.concatenate([jnp.concatenate(x, axis=1) for x in grp], axis=0)
        n_a = tiles - kt
        row_id = lax.broadcasted_iota(jnp.int32, (NB, n_a * LANES), 0) + k
        lane_id = lax.broadcasted_iota(jnp.int32, (NB, n_a * LANES), 1) + kt * LANES
        pa = panel[:, :n_a * LANES]
        pb = panel[:, n_a * LANES:]
        if kt:
            r_ref[k:k + NB, :kt * LANES] = jnp.zeros((NB, kt * LANES), jnp.float32)
        r_ref[k:k + NB, kt * LANES:] = jnp.where(lane_id >= row_id, pa / scale, 0.0)
        y_ref[k:k + NB, :(kt + 1) * LANES] = pb * scale
        if kt + 1 < tiles:
            y_ref[k:k + NB, (kt + 1) * LANES:] = jnp.zeros((NB, n - (kt + 1) * LANES), jnp.float32)
        nxt = k + NB
        if nxt < n:
            nt = nxt // LANES
            left = panel[:, (nt - kt) * LANES:n_a * LANES]
            dims = (((0,), (0,)), ((), ()))
            right = panel[:, (nt - kt) * LANES:]
            upd = lax.dot_general(left, right, dims, precision=lax.Precision.HIGHEST, preferred_element_type=jnp.float32)
            upd = upd[nxt - nt * LANES:]
            w_a = n - nt * LANES
            a[nxt:, nt * LANES:] = a[nxt:, nt * LANES:] - upd[:, :w_a]
            b[nxt:, :(kt + 1) * LANES] = b[nxt:, :(kt + 1) * LANES] - upd[:, w_a:]
        if nxt % LANES == 0:
            at = kt * LANES
            part = lax.dot_general(
                m_ref[:, :nxt], y_ref[at:nxt, :nxt], (((1,), (1,)), ((), ())),
                precision=lax.Precision.HIGHEST, preferred_element_type=jnp.float32)
            cols = basis_ref.shape[1]
            for i in range(basis_ref.shape[0]):
                basis_ref[i, :, at:nxt] = part[i * cols:(i + 1) * cols]


def factor(gram, matrix, scale, rows, cols):
    n = matrix.shape[1]
    square = jax.ShapeDtypeStruct((n, n), jnp.float32)
    vmem = pl.BlockSpec(memory_space=pltpu.VMEM)
    return pl.pallas_call(
        functools.partial(factor_kernel, scale, n),
        out_shape=(square, jax.ShapeDtypeStruct((rows, cols, n), jnp.float32)),
        in_specs=[vmem, vmem],
        out_specs=(vmem, vmem),
        scratch_shapes=[pltpu.VMEM((n, n), jnp.float32)] * 3,
        name="factor",
    )(gram, matrix)


def filter_kernel(taps, v_ref, x_ref, out_ref, flat):
    rows, cols, length = x_ref.shape
    chunks = out_ref.shape[0]
    steps = chunks * LANES
    for i in range(rows):
        flat[i * cols:(i + 1) * cols] = x_ref[i]
    lane = lax.broadcasted_iota(jnp.int32, (1, length), 1)
    row = jnp.where(lane == taps // 2, v_ref[...] + 1.0, v_ref[...])
    band = pltpu.roll(jnp.broadcast_to(row, (steps, length)), 0, 1, stride=1, stride_axis=0)
    for c in range(chunks):
        out_ref[c] = lax.dot_general(
            flat[...], band[c * LANES:(c + 1) * LANES], (((1,), (1,)), ((), ())),
            precision=lax.Precision.HIGHEST, preferred_element_type=jnp.float32)


def filtered_tiles(field, time_taps):
    rows, cols, length = field.shape
    taps = time_taps.shape[0]
    chunks = (length - taps + 1) // LANES
    row = jnp.pad(time_taps, (0, length - taps)).reshape(1, length)
    vmem = pl.BlockSpec(memory_space=pltpu.VMEM)
    return pl.pallas_call(
        functools.partial(filter_kernel, taps),
        out_shape=jax.ShapeDtypeStruct((chunks, rows * cols, LANES), jnp.float32),
        in_specs=[vmem, vmem],
        out_specs=vmem,
        scratch_shapes=[pltpu.VMEM((rows * cols, length), jnp.float32)],
        name="filter",
    )(row, field)


def halo_kernel(n_lat, n_lon, cols, taps, pieces, x_ref, w_ref, out_ref, ext, shifted, psend, precv, fsend, frecv, lsend, lrecv):
    lat, lon = lax.axis_index("lat"), lax.axis_index("lon")
    chunks, size = x_ref.shape[0], x_ref.shape[1]
    odd = lax.rem(lat, 2)
    partner = lat + 1 - 2 * odd
    target = lat + 2 - 4 * odd
    source = lat - 2 + 4 * odd
    hands_on = jnp.logical_and(target >= 0, target < n_lat)
    gets = jnp.logical_and(source >= 0, source < n_lat)
    right, left = lax.rem(lon + 1, n_lon), lax.rem(lon + n_lon - 1, n_lon)
    step = size // pieces

    barrier = pltpu.get_barrier_semaphore()
    for dev in ((partner, lon), (lat, left), (lat, right)):
        pl.semaphore_signal(barrier, inc=1, device_id=dev, device_id_type=MESH)

    @pl.when(gets)
    def _():
        pl.semaphore_signal(barrier, inc=1, device_id=(source, lon), device_id_type=MESH)

    @pl.when(hands_on)
    def _():
        pl.semaphore_signal(barrier, inc=1, device_id=(target, lon), device_id_type=MESH)

    pl.semaphore_wait(barrier, 3 + gets.astype(jnp.int32) + hands_on.astype(jnp.int32))

    far = 2 * size * odd
    near = 2 * size * (1 - odd)

    def swap(c, s):
        return pltpu.make_async_remote_copy(
            src_ref=x_ref.at[c, pl.ds(s * step, step)],
            dst_ref=ext.at[c, pl.ds(pl.multiple_of(far + s * step, 8), step)],
            send_sem=psend.at[c, s], recv_sem=precv.at[c, s], device_id=(partner, lon), device_id_type=MESH)

    def hand(c, s):
        return pltpu.make_async_remote_copy(
            src_ref=ext.at[c, pl.ds(pl.multiple_of(near + s * step, 8), step)],
            dst_ref=ext.at[c, pl.ds(pl.multiple_of(far + s * step, 8), step)],
            send_sem=fsend.at[c, s], recv_sem=frecv.at[c, s], device_id=(target, lon), device_id_type=MESH)

    def side(c, way):
        return pltpu.make_async_remote_copy(
            src_ref=out_ref.at[c, 1], dst_ref=out_ref.at[c, 2 * way],
            send_sem=lsend.at[c, way], recv_sem=lrecv.at[c, way],
            device_id=(lat, left if way else right), device_id_type=MESH)

    def relay(c, s):
        swap(c, s).wait_recv()

        @pl.when(hands_on)
        def _():
            hand(c, s).start()

    for c in range(chunks):
        for s in range(pieces):
            swap(c, s).start()
    for c in range(chunks):
        ext[c, size:2 * size] = x_ref[c]

    @pl.when(jnp.logical_not(gets))
    def _():
        for c in range(chunks):
            ext[c, pl.ds(pl.multiple_of(far, 8), size)] = jnp.zeros((size, LANES), jnp.float32)

    rows_lat = size // cols
    classes = 1
    while classes * cols % 8:
        classes *= 2
    block = classes * cols
    order = [(c, s) for c in range(chunks) for s in range(pieces)]
    at = 0
    for c in range(chunks):
        ahead = min(len(order), (c + 1) * pieces + pieces // 2)
        for p in order[at:ahead]:
            relay(*p)
        at = ahead

        @pl.when(gets)
        def _():
            for s in range(pieces):
                hand(c, s).wait_recv()

        for q in range(1, classes):
            shifted[q - 1, :3 * size - q * cols] = ext[c, q * cols:]

        def smooth(b, carry):
            acc = None
            for k in range(taps):
                place = k + rows_lat - taps // 2
                q = place % classes
                rows = pl.ds(pl.multiple_of(b * block + (place - q) * cols, 8), block)
                value = ext[c, rows] if q == 0 else shifted[q - 1, rows]
                acc = w_ref[k] * value if acc is None else acc + w_ref[k] * value
            out_ref[c, 1, pl.ds(pl.multiple_of(b * block, 8), block)] = acc
            return carry

        lax.fori_loop(0, size // block, smooth, 0)
        side(c, 0).start()
        side(c, 1).start()
    for c in range(chunks):
        for s in range(pieces):
            swap(c, s).wait_send()

    @pl.when(hands_on)
    def _():
        for c in range(chunks):
            for s in range(pieces):
                hand(c, s).wait_send()

    for c in range(chunks):
        side(c, 0).wait()
        side(c, 1).wait()


def halo(tiles, lat_kernel, cols):
    n_lat, n_lon = lax.axis_size("lat"), lax.axis_size("lon")
    chunks, size, width = tiles.shape
    classes = 1
    while classes * cols % 8:
        classes *= 2
    pieces = next(p for p in (5, 4, 2, 1) if size % (8 * p) == 0)
    dma = pltpu.SemaphoreType.DMA
    vmem = pl.BlockSpec(memory_space=pltpu.VMEM)
    return pl.pallas_call(
        functools.partial(halo_kernel, n_lat, n_lon, cols, lat_kernel.shape[0], pieces),
        out_shape=jax.ShapeDtypeStruct((chunks, 3, size, width), jnp.float32),
        in_specs=[vmem, pl.BlockSpec(memory_space=pltpu.SMEM)],
        out_specs=vmem,
        scratch_shapes=[
            pltpu.VMEM((chunks, 3 * size, width), jnp.float32),
            pltpu.VMEM((max(1, classes - 1), 3 * size, width), jnp.float32),
        ] + [dma((chunks, pieces))] * 4 + [dma((chunks, 2))] * 2,
        compiler_params=pltpu.CompilerParams(collective_id=1, has_side_effects=True),
        name="halo",
    )(tiles, lat_kernel)


def gram_kernel(cols, group, x_ref, lon_ref, w_ref, m_ref, g_ref):
    chunks, parts, size, width = x_ref.shape
    taps = lon_ref.shape[0]
    rows = group * cols
    first_row = lax.axis_index("lat") * (size // cols)
    shape = (rows, parts * rows)
    r, e = lax.broadcasted_iota(jnp.int32, shape, 0), lax.broadcasted_iota(jnp.int32, shape, 1)
    part = sum((e >= p * rows).astype(jnp.int32) for p in range(1, parts)) + jnp.zeros(shape, jnp.int32)
    e = e - part * rows
    er = sum((e >= q * cols).astype(jnp.int32) for q in range(1, group)) + jnp.zeros(shape, jnp.int32)
    rr = sum((r >= q * cols).astype(jnp.int32) for q in range(1, group)) + jnp.zeros(shape, jnp.int32)
    offset = part * cols + (e - er * cols) - (r - rr * cols) - (cols - taps // 2)
    offset = jnp.where(er == rr, offset, -1)
    band = jnp.zeros(shape, jnp.float32)
    for k in range(taps):
        band = jnp.where(offset == k, lon_ref[k], band)
    which = rr[:, :1] + jnp.zeros((rows, chunks * width), jnp.int32)
    for g in range(size // rows):
        at = slice(g * rows, (g + 1) * rows)
        value = jnp.concatenate(
            [jnp.concatenate([x_ref[c, p, at] for c in range(chunks)], axis=1) for p in range(parts)], axis=0)
        value = jnp.dot(band, value, precision=lax.Precision.HIGHEST, preferred_element_type=jnp.float32)
        weight = jnp.zeros(value.shape, jnp.float32)
        for q in range(group):
            weight = jnp.where(which == q, w_ref[first_row + g * group + q], weight)
        m_ref[at] = value * weight
    steps = chunks * width
    at = 0
    for t in range(0, steps, LANES):
        left = m_ref[:, t:t + LANES]
        both = lax.dot_general(
            left, m_ref[:, t:], (((0,), (0,)), ((), ())),
            precision=lax.Precision.HIGHEST, preferred_element_type=jnp.float32)
        for q in range(0, steps - t, LANES):
            g_ref[at:at + LANES] = both[:, q:q + LANES]
            at += LANES


def matrix_and_gram(ext, lon_kernel, weights, cols):
    chunks, parts, size, width = ext.shape
    rows_lat = size // cols
    group = max(q for q in range(1, rows_lat + 1) if rows_lat % q == 0 and q * cols % 8 == 0 and (q * cols <= 96 or q == rows_lat))
    group = min([q for q in range(1, rows_lat + 1) if rows_lat % q == 0 and q * cols % 8 == 0 and 64 <= q * cols] or [group])
    vmem, smem = pl.BlockSpec(memory_space=pltpu.VMEM), pl.BlockSpec(memory_space=pltpu.SMEM)
    steps = chunks * width
    tiles = steps // LANES
    packed = LANES * tiles * (tiles + 1) // 2
    return pl.pallas_call(
        functools.partial(gram_kernel, cols, group),
        out_shape=(jax.ShapeDtypeStruct((size, steps), jnp.float32), jax.ShapeDtypeStruct((packed, LANES), jnp.float32)),
        in_specs=[vmem, smem, smem],
        out_specs=(vmem, vmem),
        name="matrix_gram",
    )(ext, lon_kernel, weights)


def body(field, lat_kernel, lon_kernel, time_taps):
    rows_lat, rows_lon = field.shape[:2]
    total_lat = rows_lat * lax.axis_size("lat")
    cells = total_lat * rows_lon * lax.axis_size("lon")
    tiles = filtered_tiles(field, time_taps)
    ext = halo(tiles, lat_kernel, rows_lon)
    latitude = np.pi * (np.arange(total_lat) + 0.5) / total_lat - np.pi / 2
    weights = jnp.asarray(np.sqrt(np.cos(latitude)), jnp.float32)
    matrix, local_gram = matrix_and_gram(ext, lon_kernel, weights, rows_lon)
    gram = sum_over_mesh(local_gram)
    upper, basis = factor(gram, matrix, float(cells) ** 0.5, rows_lat, rows_lon)
    return (basis, upper)


def solution(mesh):
    placed = (P("lat", "lon", None), P(), P(), P())
    return jax.shard_map(
        body, mesh=mesh, in_specs=placed, out_specs=(P("lat", "lon", None), P()), check_vma=False
    )
```

```python
import functools

import jax
import jax.numpy as jnp
import numpy as np
from jax import lax
from jax.experimental import pallas as pl
from jax.experimental.pallas import tpu as pltpu
from jax.sharding import PartitionSpec as P


MESH = pl.DeviceIdType.MESH
NB = 32
LANES = 128


def sum_kernel(n_lat, n_lon, pair, cols, group, x_ref, lon_ref, w_ref, m_ref, out_ref, g_ref, rbuf, zbuf, ssem, rsem, zssem, zrsem, cssem, crsem):
    lat, lon = lax.axis_index("lat"), lax.axis_index("lon")
    n_p, n_z = n_lat * pair, n_lon // pair
    rows = g_ref.shape[0] // n_p
    core, z = lax.rem(lon, pair), lon // pair
    me = lat * pair + core

    def plane_peer(o):
        peer = lax.rem(me + o, n_p)
        return peer, (peer // pair, z * pair + lax.rem(peer, pair))

    def z_peer(o):
        return (lat, lax.rem(z + o, n_z) * pair + core)

    barrier = pltpu.get_barrier_semaphore()
    for o in range(1, n_p):
        pl.semaphore_signal(barrier, inc=1, device_id=plane_peer(o)[1], device_id_type=MESH)
    for o in range(1, n_z):
        pl.semaphore_signal(barrier, inc=1, device_id=z_peer(o), device_id_type=MESH)
    gram_kernel(cols, group, x_ref, lon_ref, w_ref, m_ref, g_ref)
    pl.semaphore_wait(barrier, n_p + n_z - 2)

    copies = []
    for o in range(1, n_p):
        peer, dev = plane_peer(o)
        c = pltpu.make_async_remote_copy(
            src_ref=g_ref.at[pl.ds(pl.multiple_of(peer * rows, 8), rows)], dst_ref=rbuf.at[o],
            send_sem=ssem.at[o], recv_sem=rsem.at[o], device_id=dev, device_id_type=MESH)
        c.start()
        copies.append(c)
    mine = pl.ds(pl.multiple_of(me * rows, 8), rows)
    acc = g_ref[mine, :]
    for o in range(1, n_p):
        copies[o - 1].wait_recv()
        acc = acc + rbuf[o]
    for c in copies:
        c.wait_send()
    zbuf[z] = acc

    copies = []
    for o in range(1, n_z):
        c = pltpu.make_async_remote_copy(
            src_ref=zbuf.at[z], dst_ref=zbuf.at[z],
            send_sem=zssem.at[o], recv_sem=zrsem.at[o], device_id=z_peer(o), device_id_type=MESH)
        c.start()
        copies.append(c)
    for c in copies:
        c.wait()
    total = zbuf[0]
    for k in range(1, n_z):
        total = total + zbuf[k]
    out_ref[mine, :] = total

    copies = []
    for o in range(1, n_p):
        c = pltpu.make_async_remote_copy(
            src_ref=out_ref.at[mine], dst_ref=out_ref.at[mine],
            send_sem=cssem.at[o], recv_sem=crsem.at[o], device_id=plane_peer(o)[1], device_id_type=MESH)
        c.start()
        copies.append(c)
    for c in copies:
        c.wait()


def factor_kernel(scale, n, g_ref, m_ref, r_ref, basis_ref, a, b, y_ref):
    at = 0
    for t in range(0, n, LANES):
        if t:
            a[t:t + LANES, :t] = jnp.zeros((LANES, t), jnp.float32)
        for q in range(t, n, LANES):
            a[t:t + LANES, q:q + LANES] = g_ref[at:at + LANES]
            at += LANES
    b[...] = (lax.broadcasted_iota(jnp.int32, (n, n), 0) == lax.broadcasted_iota(jnp.int32, (n, n), 1)).astype(jnp.float32)
    sub = lax.broadcasted_iota(jnp.int32, (8, LANES), 0)
    tiles = n // LANES
    for k in range(0, n, NB):
        kt = k // LANES
        live = [(a, t) for t in range(kt, tiles)] + [(b, t) for t in range(kt + 1)]
        grp = [[ref[k + 8 * h:k + 8 * h + 8, t * LANES:(t + 1) * LANES] for ref, t in live] for h in range(NB // 8)]
        for g in range(NB // 8):
            hs = range(g, NB // 8)
            lane = k + 8 * g - kt * LANES
            cols = [{h: jnp.broadcast_to(grp[h][0][:, lane + q:lane + q + 1], (8, LANES)) for h in hs} for q in range(8)]
            done = None
            for q in range(8):
                d = jnp.broadcast_to(cols[q][g][q:q + 1, :], (8, LANES))
                inv = 1.0 / d
                u = {h: cols[q][h] * inv for h in hs}
                u[g] = jnp.where(sub > q, u[g], 0.0)
                for p in range(q + 1, 8):
                    e = jnp.broadcast_to(cols[p][g][q:q + 1, :], (8, LANES))
                    for h in hs:
                        cols[p][h] = cols[p][h] - u[h] * e
                root = lax.sqrt(d)
                done = root if done is None else jnp.where(sub == q, root, done)
                for t in range(len(live)):
                    row = jnp.broadcast_to(grp[g][t][q:q + 1, :], (8, LANES))
                    for h in hs:
                        grp[h][t] = grp[h][t] - u[h] * row
            rinv = 1.0 / done
            for t in range(len(live)):
                grp[g][t] = grp[g][t] * rinv
        panel = jnp.concatenate([jnp.concatenate(x, axis=1) for x in grp], axis=0)
        n_a = tiles - kt
        row_id = lax.broadcasted_iota(jnp.int32, (NB, n_a * LANES), 0) + k
        lane_id = lax.broadcasted_iota(jnp.int32, (NB, n_a * LANES), 1) + kt * LANES
        pa = panel[:, :n_a * LANES]
        pb = panel[:, n_a * LANES:]
        if kt:
            r_ref[k:k + NB, :kt * LANES] = jnp.zeros((NB, kt * LANES), jnp.float32)
        r_ref[k:k + NB, kt * LANES:] = jnp.where(lane_id >= row_id, pa / scale, 0.0)
        y_ref[k:k + NB, :(kt + 1) * LANES] = pb * scale
        if kt + 1 < tiles:
            y_ref[k:k + NB, (kt + 1) * LANES:] = jnp.zeros((NB, n - (kt + 1) * LANES), jnp.float32)
        nxt = k + NB
        if nxt < n:
            nt = nxt // LANES
            left = panel[:, (nt - kt) * LANES:n_a * LANES]
            dims = (((0,), (0,)), ((), ()))
            right = panel[:, (nt - kt) * LANES:]
            upd = lax.dot_general(left, right, dims, precision=lax.Precision.HIGHEST, preferred_element_type=jnp.float32)
            upd = upd[nxt - nt * LANES:]
            w_a = n - nt * LANES
            a[nxt:, nt * LANES:] = a[nxt:, nt * LANES:] - upd[:, :w_a]
            b[nxt:, :(kt + 1) * LANES] = b[nxt:, :(kt + 1) * LANES] - upd[:, w_a:]
        if nxt % LANES == 0:
            at = kt * LANES
            part = lax.dot_general(
                m_ref[:, :nxt], y_ref[at:nxt, :nxt], (((1,), (1,)), ((), ())),
                precision=lax.Precision.HIGHEST, preferred_element_type=jnp.float32)
            cols = basis_ref.shape[1]
            for i in range(basis_ref.shape[0]):
                basis_ref[i, :, at:nxt] = part[i * cols:(i + 1) * cols]


def factor(gram, matrix, scale, rows, cols):
    n = matrix.shape[1]
    square = jax.ShapeDtypeStruct((n, n), jnp.float32)
    vmem = pl.BlockSpec(memory_space=pltpu.VMEM)
    return pl.pallas_call(
        functools.partial(factor_kernel, scale, n),
        out_shape=(square, jax.ShapeDtypeStruct((rows, cols, n), jnp.float32)),
        in_specs=[vmem, vmem],
        out_specs=(vmem, vmem),
        scratch_shapes=[pltpu.VMEM((n, n), jnp.float32)] * 3,
        name="factor",
    )(gram, matrix)


def filter_kernel(taps, v_ref, x_ref, out_ref, flat, row_ref):
    rows, cols, length = x_ref.shape
    chunks = out_ref.shape[0]
    steps = chunks * LANES
    for i in range(rows):
        flat[i * cols:(i + 1) * cols] = x_ref[i]
    lane = lax.broadcasted_iota(jnp.int32, (1, length), 1)
    row_ref[...] = jnp.zeros((1, length), jnp.float32)
    row_ref[:, :taps] = v_ref[...].reshape(1, taps)
    row = jnp.where(lane == taps // 2, row_ref[...] + 1.0, row_ref[...])
    band = pltpu.roll(jnp.broadcast_to(row, (steps, length)), 0, 1, stride=1, stride_axis=0)
    for c in range(chunks):
        out_ref[c] = lax.dot_general(
            flat[...], band[c * LANES:(c + 1) * LANES], (((1,), (1,)), ((), ())),
            precision=lax.Precision.HIGHEST, preferred_element_type=jnp.float32)


def filtered_tiles(field, time_taps):
    rows, cols, length = field.shape
    taps = time_taps.shape[0]
    chunks = (length - taps + 1) // LANES
    vmem = pl.BlockSpec(memory_space=pltpu.VMEM)
    return pl.pallas_call(
        functools.partial(filter_kernel, taps),
        out_shape=jax.ShapeDtypeStruct((chunks, rows * cols, LANES), jnp.float32),
        in_specs=[vmem, vmem],
        out_specs=vmem,
        scratch_shapes=[pltpu.VMEM((rows * cols, length), jnp.float32), pltpu.VMEM((1, length), jnp.float32)],
        name="filter",
    )(time_taps, field)


def halo_kernel(n_lat, n_lon, cols, taps, pieces, x_ref, w_ref, out_ref, ext, shifted, psend, precv, fsend, frecv, lsend, lrecv):
    lat, lon = lax.axis_index("lat"), lax.axis_index("lon")
    chunks, size = x_ref.shape[0], x_ref.shape[1]
    odd = lax.rem(lat, 2)
    partner = lat + 1 - 2 * odd
    target = lat + 2 - 4 * odd
    source = lat - 2 + 4 * odd
    hands_on = jnp.logical_and(target >= 0, target < n_lat)
    gets = jnp.logical_and(source >= 0, source < n_lat)
    right, left = lax.rem(lon + 1, n_lon), lax.rem(lon + n_lon - 1, n_lon)
    step = size // pieces

    barrier = pltpu.get_barrier_semaphore()
    for dev in ((partner, lon), (lat, left), (lat, right)):
        pl.semaphore_signal(barrier, inc=1, device_id=dev, device_id_type=MESH)

    @pl.when(gets)
    def _():
        pl.semaphore_signal(barrier, inc=1, device_id=(source, lon), device_id_type=MESH)

    @pl.when(hands_on)
    def _():
        pl.semaphore_signal(barrier, inc=1, device_id=(target, lon), device_id_type=MESH)

    pl.semaphore_wait(barrier, 3 + gets.astype(jnp.int32) + hands_on.astype(jnp.int32))

    far = 2 * size * odd
    near = 2 * size * (1 - odd)

    def swap(c, s):
        return pltpu.make_async_remote_copy(
            src_ref=x_ref.at[c, pl.ds(s * step, step)],
            dst_ref=ext.at[c, pl.ds(pl.multiple_of(far + s * step, 8), step)],
            send_sem=psend.at[c, s], recv_sem=precv.at[c, s], device_id=(partner, lon), device_id_type=MESH)

    def hand(c, s):
        return pltpu.make_async_remote_copy(
            src_ref=ext.at[c, pl.ds(pl.multiple_of(near + s * step, 8), step)],
            dst_ref=ext.at[c, pl.ds(pl.multiple_of(far + s * step, 8), step)],
            send_sem=fsend.at[c, s], recv_sem=frecv.at[c, s], device_id=(target, lon), device_id_type=MESH)

    def side(c, way):
        return pltpu.make_async_remote_copy(
            src_ref=out_ref.at[c, 1], dst_ref=out_ref.at[c, 2 * way],
            send_sem=lsend.at[c, way], recv_sem=lrecv.at[c, way],
            device_id=(lat, left if way else right), device_id_type=MESH)

    def relay(c, s):
        swap(c, s).wait_recv()

        @pl.when(hands_on)
        def _():
            hand(c, s).start()

    for c in range(chunks):
        for s in range(pieces):
            swap(c, s).start()
    for c in range(chunks):
        ext[c, size:2 * size] = x_ref[c]

    @pl.when(jnp.logical_not(gets))
    def _():
        for c in range(chunks):
            ext[c, pl.ds(pl.multiple_of(far, 8), size)] = jnp.zeros((size, LANES), jnp.float32)

    rows_lat = size // cols
    classes = 1
    while classes * cols % 8:
        classes *= 2
    block = classes * cols
    order = [(c, s) for c in range(chunks) for s in range(pieces)]
    at = 0
    for c in range(chunks):
        ahead = min(len(order), (c + 1) * pieces + pieces // 2)
        for p in order[at:ahead]:
            relay(*p)
        at = ahead

        @pl.when(gets)
        def _():
            for s in range(pieces):
                hand(c, s).wait_recv()

        for q in range(1, classes):
            shifted[q - 1, :3 * size - q * cols] = ext[c, q * cols:]

        def smooth(b, carry):
            acc = None
            for k in range(taps):
                place = k + rows_lat - taps // 2
                q = place % classes
                rows = pl.ds(pl.multiple_of(b * block + (place - q) * cols, 8), block)
                value = ext[c, rows] if q == 0 else shifted[q - 1, rows]
                acc = w_ref[k] * value if acc is None else acc + w_ref[k] * value
            out_ref[c, 1, pl.ds(pl.multiple_of(b * block, 8), block)] = acc
            return carry

        lax.fori_loop(0, size // block, smooth, 0)
        side(c, 0).start()
        side(c, 1).start()
    for c in range(chunks):
        for s in range(pieces):
            swap(c, s).wait_send()

    @pl.when(hands_on)
    def _():
        for c in range(chunks):
            for s in range(pieces):
                hand(c, s).wait_send()

    for c in range(chunks):
        side(c, 0).wait()
        side(c, 1).wait()


def halo(tiles, lat_kernel, cols):
    n_lat, n_lon = lax.axis_size("lat"), lax.axis_size("lon")
    chunks, size, width = tiles.shape
    classes = 1
    while classes * cols % 8:
        classes *= 2
    pieces = next(p for p in (5, 4, 2, 1) if size % (8 * p) == 0)
    dma = pltpu.SemaphoreType.DMA
    vmem = pl.BlockSpec(memory_space=pltpu.VMEM)
    return pl.pallas_call(
        functools.partial(halo_kernel, n_lat, n_lon, cols, lat_kernel.shape[0], pieces),
        out_shape=jax.ShapeDtypeStruct((chunks, 3, size, width), jnp.float32),
        in_specs=[vmem, pl.BlockSpec(memory_space=pltpu.SMEM)],
        out_specs=vmem,
        scratch_shapes=[
            pltpu.VMEM((chunks, 3 * size, width), jnp.float32),
            pltpu.VMEM((max(1, classes - 1), 3 * size, width), jnp.float32),
        ] + [dma((chunks, pieces))] * 4 + [dma((chunks, 2))] * 2,
        compiler_params=pltpu.CompilerParams(collective_id=1, has_side_effects=True),
        name="halo",
    )(tiles, lat_kernel)


def gram_kernel(cols, group, x_ref, lon_ref, w_ref, m_ref, g_ref):
    chunks, parts, size, width = x_ref.shape
    taps = lon_ref.shape[0]
    rows = group * cols
    first_row = lax.axis_index("lat") * (size // cols)
    shape = (rows, parts * rows)
    r, e = lax.broadcasted_iota(jnp.int32, shape, 0), lax.broadcasted_iota(jnp.int32, shape, 1)
    part = sum((e >= p * rows).astype(jnp.int32) for p in range(1, parts)) + jnp.zeros(shape, jnp.int32)
    e = e - part * rows
    er = sum((e >= q * cols).astype(jnp.int32) for q in range(1, group)) + jnp.zeros(shape, jnp.int32)
    rr = sum((r >= q * cols).astype(jnp.int32) for q in range(1, group)) + jnp.zeros(shape, jnp.int32)
    offset = part * cols + (e - er * cols) - (r - rr * cols) - (cols - taps // 2)
    offset = jnp.where(er == rr, offset, -1)
    band = jnp.zeros(shape, jnp.float32)
    for k in range(taps):
        band = jnp.where(offset == k, lon_ref[k], band)
    which = rr[:, :1] + jnp.zeros((rows, chunks * width), jnp.int32)
    for g in range(size // rows):
        at = slice(g * rows, (g + 1) * rows)
        value = jnp.concatenate(
            [jnp.concatenate([x_ref[c, p, at] for c in range(chunks)], axis=1) for p in range(parts)], axis=0)
        value = jnp.dot(band, value, precision=lax.Precision.HIGHEST, preferred_element_type=jnp.float32)
        weight = jnp.zeros(value.shape, jnp.float32)
        for q in range(group):
            weight = jnp.where(which == q, w_ref[first_row + g * group + q], weight)
        m_ref[at] = value * weight
    steps = chunks * width
    at = 0
    for t in range(0, steps, LANES):
        left = m_ref[:, t:t + LANES]
        both = lax.dot_general(
            left, m_ref[:, t:], (((0,), (0,)), ((), ())),
            precision=lax.Precision.HIGHEST, preferred_element_type=jnp.float32)
        for q in range(0, steps - t, LANES):
            g_ref[at:at + LANES] = both[:, q:q + LANES]
            at += LANES


def matrix_and_gram(ext, lon_kernel, weights, cols):
    chunks, parts, size, width = ext.shape
    rows_lat = size // cols
    group = max(q for q in range(1, rows_lat + 1) if rows_lat % q == 0 and q * cols % 8 == 0 and (q * cols <= 96 or q == rows_lat))
    group = min([q for q in range(1, rows_lat + 1) if rows_lat % q == 0 and q * cols % 8 == 0 and 64 <= q * cols] or [group])
    vmem, smem = pl.BlockSpec(memory_space=pltpu.VMEM), pl.BlockSpec(memory_space=pltpu.SMEM)
    steps = chunks * width
    tiles = steps // LANES
    packed = LANES * tiles * (tiles + 1) // 2
    n_lat, n_lon = lax.axis_size("lat"), lax.axis_size("lon")
    pair = 2 if n_lon % 2 == 0 else 1
    n_p, n_z = n_lat * pair, n_lon // pair
    share = packed // n_p
    dma = pltpu.SemaphoreType.DMA
    return pl.pallas_call(
        functools.partial(sum_kernel, n_lat, n_lon, pair, cols, group),
        out_shape=(jax.ShapeDtypeStruct((size, steps), jnp.float32), jax.ShapeDtypeStruct((packed, LANES), jnp.float32)),
        in_specs=[vmem, smem, smem],
        out_specs=(vmem, vmem),
        scratch_shapes=[
            pltpu.VMEM((packed, LANES), jnp.float32),
            pltpu.VMEM((n_p, share, LANES), jnp.float32),
            pltpu.VMEM((n_z, share, LANES), jnp.float32),
            dma((n_p,)), dma((n_p,)), dma((n_z,)), dma((n_z,)), dma((n_p,)), dma((n_p,)),
        ],
        compiler_params=pltpu.CompilerParams(collective_id=0, has_side_effects=True),
        name="gram_sum",
    )(ext, lon_kernel, weights)


def body(field, lat_kernel, lon_kernel, time_taps):
    rows_lat, rows_lon = field.shape[:2]
    total_lat = rows_lat * lax.axis_size("lat")
    cells = total_lat * rows_lon * lax.axis_size("lon")
    tiles = filtered_tiles(field, time_taps)
    ext = halo(tiles, lat_kernel, rows_lon)
    latitude = np.pi * (np.arange(total_lat) + 0.5) / total_lat - np.pi / 2
    weights = jnp.asarray(np.sqrt(np.cos(latitude)), jnp.float32)
    matrix, gram = matrix_and_gram(ext, lon_kernel, weights, rows_lon)
    upper, basis = factor(gram, matrix, float(cells) ** 0.5, rows_lat, rows_lon)
    return (basis, upper)


def solution(mesh):
    placed = (P("lat", "lon", None), P(), P(), P())
    return jax.shard_map(
        body, mesh=mesh, in_specs=placed, out_specs=(P("lat", "lon", None), P()), check_vma=False
    )
```
